32 devices in a mesh: dp: 16 (over z, x, core), tensor: 2 (over y).
Axes of the slice: x: 2, y: 2, z: 4, core: 2. Of those that a mesh axis runs over, the one named last changes fastest.
Arguments:
- patches: float32 [1280, 4096], P('tensor', 'dp'), may hold values from -33 to 33
- in_projection: float32 [1280, 3, 1280], P('dp', None, 'tensor'), may hold values from -0.18727069 to 0.18727069
- cotangent: float32 [1280, 4096], P('tensor', 'dp'), may hold values from -6 to 6
- image_lengths: int32 [256], P('dp'), may hold values from 0 to 192, as said below
Outputs:
- attention_rows: float32 [1280, 4096], P('tensor', 'dp')
- projected_gradients: float32 [3, 1280, 4096], P(None, 'tensor', 'dp')
- weight_gradient: float32 [1280, 3, 1280], P('dp', None, 'tensor')
The draws below stay inside these ranges and needn't reach their ends.
Inputs may be any that keep to these rules, and one draw needn't show every extreme that they name: `image_lengths`: on each index of dp the 16 entries sum to 256; zero entries come last.
All inputs are finite; a program needn't handle non-finite values.
Results may differ from the reference program's by a relative error of at most 0.0003.
Values sent between devices are 32-bit elements; how exact they have to be, the bound alone decides.
No kernel may reach another device: no remote copies, remote signals or barrier semaphores. Data moves between devices by JAX's collectives and lax.ppermute only.
A program may use at most 64 MiB of HBM per device.

```python
import math
import jax
import jax.numpy as jnp
from jax import lax

D = 1280
HEAD_DIM = 80
TOK_DEV = 256
IMGS = 16
TOKENS = 4096
IMG_SLOTS = 256


def draw_patches(key, part):
    normal_part = jnp.clip(jax.random.normal(key, (TOKENS, D), jnp.float32), -5.0, 5.0)
    return jnp.transpose(normal_part)


def draw_in_projection(key, part):
    normal_part = jnp.clip(jax.random.normal(key, (D, 3, D), jnp.float32), -5.0, 5.0) / math.sqrt(D)
    return normal_part


def draw_image_lengths(key, part):
    ranks = IMG_SLOTS // IMGS
    half = ranks // 2
    capacity = TOK_DEV // 4
    head_rows = TOK_DEV - capacity
    subkeys = jax.random.split(jax.random.fold_in(key, 5), 5)
    side = jax.random.randint(subkeys[0], (half,), 0, 2, dtype=jnp.int32)
    rank_index = jnp.arange(ranks, dtype=jnp.int32)
    is_heavy = (rank_index >= half).astype(jnp.int32) == side[rank_index % half]
    head_cut = jax.random.randint(subkeys[1], (ranks, 1), TOK_DEV // 8, head_rows - TOK_DEV // 8 + 1, dtype=jnp.int32)
    whole_head = (jax.random.randint(subkeys[2], (ranks,), 0, 2, dtype=jnp.int32) == 0) | (rank_index % half == 0)
    tail_cut = jax.random.randint(subkeys[3], (ranks, 1), capacity // 4, capacity - capacity // 4 + 1, dtype=jnp.int32)
    slot_index = jnp.arange(IMGS, dtype=jnp.int32)[None, :]
    zero_row = jnp.zeros((ranks, IMGS), jnp.int32)
    whole_row = jnp.where(slot_index == 0, head_rows, jnp.where(slot_index == 1, tail_cut, jnp.where(slot_index == 2, capacity - tail_cut, zero_row)))
    split_row = jnp.where(slot_index == 0, head_cut, jnp.where(slot_index == 1, head_rows - head_cut, jnp.where(slot_index == 2, tail_cut, jnp.where(slot_index == 3, capacity - tail_cut, zero_row))))
    unit_rows = 2 * TOK_DEV // IMGS
    first_part = jax.random.randint(subkeys[4], (ranks, IMGS // 2), 1, unit_rows, dtype=jnp.int32)
    light_row = jnp.stack([first_part, unit_rows - first_part], axis=2).reshape(ranks, IMGS)
    heavy_row = jnp.where(whole_head[:, None], whole_row, split_row)
    chosen = jnp.where(is_heavy[:, None], heavy_row, light_row)
    return chosen.reshape(-1).astype(jnp.int32)


def block_levels(stream_key, shape, cuts, smallest, largest):
    gain = 1.0
    for axis_at, shards_of in cuts:
        draws = jax.random.uniform(jax.random.fold_in(jax.random.fold_in(stream_key, 6), axis_at), (shards_of,), jnp.float32, smallest / len(cuts), largest / len(cuts))
        gain = gain * jnp.repeat(jnp.exp(draws), shape[axis_at] // shards_of).reshape((-1,) + (1,) * (len(shape) - 1 - axis_at))
    return gain


def gaussian(key, dims, scale, bound, cuts=(), kind=jnp.bfloat16):
    values = jax.random.normal(key, dims, jnp.float32) * scale
    if len(cuts) > 0:
        values = block_levels(key, dims, cuts, -0.22, 0.18) * values
    return jnp.clip(values, min=-bound, max=bound).astype(kind)


def setup_inputs(seed: int = 0) -> dict:
    splits = jax.random.split(jax.random.key(seed), 5)
    return {
        "patches": draw_patches(jax.random.fold_in(splits[4], 71), 0),
        "in_projection": draw_in_projection(jax.random.fold_in(splits[4], 71), 0),
        "cotangent": gaussian(splits[2], (D, TOKENS), 1.0, 6.0, ((0, 2), (1, 16)), jnp.float32),
        "image_lengths": draw_image_lengths(jax.random.fold_in(splits[4], 71), 0),
    }


HIGHEST_PRECISION = lax.Precision.HIGHEST
MASKED_SCORE = -1e+30

def attend(query_rows, key_rows, value_rows, same_image):
    count = query_rows.shape[0]
    heads_here = query_rows.shape[1] // HEAD_DIM
    shaped_query = query_rows.reshape(count, heads_here, HEAD_DIM)
    shaped_key = key_rows.reshape(count, heads_here, HEAD_DIM)
    shaped_value = value_rows.reshape(count, heads_here, HEAD_DIM)
    scores = jnp.einsum('qhd,khd->hqk', shaped_query, shaped_key, precision=HIGHEST_PRECISION) * HEAD_DIM ** (-0.5)
    scores = jnp.where(same_image[None], scores, MASKED_SCORE)
    weights = jax.nn.softmax(scores, axis=-1)
    mixed = jnp.einsum('hqk,khd->qhd', weights, shaped_value, precision=HIGHEST_PRECISION)
    return mixed.reshape(count, heads_here * HEAD_DIM)

def reference(patches, in_projection, cotangent, image_lengths):
    patch_rows = jnp.transpose(patches)
    upstream = jnp.transpose(cotangent)
    token_count = patch_rows.shape[0]
    rank_count = token_count // TOK_DEV
    projected = jnp.dot(patch_rows, in_projection.reshape(D, 3 * D), precision=HIGHEST_PRECISION, preferred_element_type=jnp.float32)

    def one_rank(rank):
        offset = rank * TOK_DEV
        rows_here = lax.dynamic_slice_in_dim(projected, offset, TOK_DEV, 0)
        grads_here = lax.dynamic_slice_in_dim(upstream, offset, TOK_DEV, 0)
        lengths = lax.dynamic_slice_in_dim(image_lengths, rank * IMGS, IMGS, 0)
        ends = jnp.cumsum(lengths, dtype=jnp.int32)
        positions = jnp.arange(TOK_DEV, dtype=jnp.int32)
        image_index = lax.optimization_barrier(jnp.sum((positions[:, None] >= ends[None, :]).astype(jnp.int32), axis=1))
        same_image = image_index[:, None] == image_index[None, :]

        def inner(query_rows, key_rows, value_rows):
            return attend(query_rows, key_rows, value_rows, same_image)
        mixed, pullback = jax.vjp(inner, rows_here[:, :D], rows_here[:, D:2 * D], rows_here[:, 2 * D:])
        query_grad, key_grad, value_grad = pullback(grads_here)
        return (mixed, jnp.stack([query_grad, key_grad, value_grad]))
    mixed_all, grads_all = lax.map(one_rank, jnp.arange(rank_count, dtype=jnp.int32))
    mixed_rows = mixed_all.reshape(token_count, D)
    grad_rows = jnp.transpose(grads_all, (1, 0, 2, 3)).reshape(3, token_count, D)
    flattened = jnp.concatenate([grad_rows[0], grad_rows[1], grad_rows[2]], axis=1)
    weight_gradient = jnp.dot(patches, flattened, precision=HIGHEST_PRECISION, preferred_element_type=jnp.float32).reshape(D, 3, D)
    return (jnp.transpose(mixed_rows), jnp.transpose(grad_rows, (0, 2, 1)), weight_gradient)
```

```python
import functools

import jax
import jax.numpy as jnp
from jax import lax
from jax.experimental import pallas as pl
from jax.experimental.pallas import tpu as pltpu
from jax.sharding import PartitionSpec as P

HEAD_DIM = 80
BLOCK = 128


HIGHEST_PRECISION = lax.Precision.HIGHEST
MASKED_SCORE = -1e30
VMEM_LIMIT = 48 * 1024 * 1024


def from_partner(value, axis, stride):
    return lax.ppermute(value, axis, [(i, i ^ 1 << stride) for i in range(lax.axis_size(axis))])


def image_bounds(image_lengths, row_count):
    image_ends = jnp.cumsum(image_lengths, dtype=jnp.int32)
    image_starts = image_ends - image_lengths
    positions = jnp.arange(row_count, dtype=jnp.int32)
    inside = (positions[:, None] >= image_starts[None, :]) & (
        positions[:, None] < image_ends[None, :]
    )
    row_begin = jnp.sum(jnp.where(inside, image_starts[None, :], 0), axis=1)
    row_finish = jnp.sum(jnp.where(inside, image_ends[None, :], 0), axis=1)
    return (image_starts, row_begin, row_finish)


def gather_features(local_rows):
    return lax.all_gather(local_rows, "tensor", axis=1, tiled=True)


def project(whole_rows, in_projection):
    width_all = in_projection.shape[1] * in_projection.shape[2]
    piece = lax.all_gather(in_projection, "dp", axis=0, tiled=True)
    flat_piece = piece.reshape(piece.shape[0], width_all)
    return jnp.dot(
        whole_rows, flat_piece, precision=HIGHEST_PRECISION, preferred_element_type=jnp.float32
    )


def attend_blocks(query_all, key_all, value_all, grad_all, work_begin, work_finish, work_valid):
    work_rows, width_dev = query_all.shape
    heads_here = width_dev // HEAD_DIM
    scale = HEAD_DIM ** (-0.5)
    block_count = work_rows // BLOCK

    def by_heads(array):
        return array.reshape(array.shape[0], heads_here, HEAD_DIM)

    def block_rows(array, index):
        return lax.dynamic_slice_in_dim(array, index * BLOCK, BLOCK, 0)

    def one_block(block_index, carried):
        out_all, dq_all, dk_all, dv_all = carried
        query_block = by_heads(block_rows(query_all, block_index))
        grad_block = by_heads(block_rows(grad_all, block_index))
        begin_block = block_rows(work_begin, block_index)
        finish_block = block_rows(work_finish, block_index)
        valid_block = block_rows(work_valid, block_index)
        lowest = jnp.min(jnp.where(valid_block, begin_block, work_rows)) // BLOCK
        highest = jnp.where(
            jnp.any(valid_block),
            (jnp.max(jnp.where(valid_block, finish_block, 0)) - 1) // BLOCK,
            -1,
        )

        def tile_scores(tile_index):
            key_tile = by_heads(block_rows(key_all, tile_index))
            value_tile = by_heads(block_rows(value_all, tile_index))
            allowed = (
                begin_block[:, None] == block_rows(work_begin, tile_index)[None, :]
            ) & valid_block[:, None]
            scores = (
                jnp.einsum("qhd,khd->hqk", query_block, key_tile, precision=HIGHEST_PRECISION)
                * scale
            )
            return (key_tile, value_tile, allowed[None], scores)

        def forward(tile_index, state):
            peak, total, accum = state
            key_tile, value_tile, allowed, scores = tile_scores(tile_index)
            scores = jnp.where(allowed, scores, MASKED_SCORE)
            new_peak = jnp.maximum(peak, jnp.max(scores, axis=2))
            probs = jnp.where(allowed, jnp.exp(scores - new_peak[:, :, None]), 0.0)
            shrink = jnp.exp(peak - new_peak)
            total = total * shrink + jnp.sum(probs, axis=2)
            accum = accum * jnp.transpose(shrink)[:, :, None] + jnp.einsum(
                "hqk,khd->qhd", probs, value_tile, precision=HIGHEST_PRECISION
            )
            return (new_peak, total, accum)

        start_state = (
            jnp.full((heads_here, BLOCK), MASKED_SCORE, jnp.float32),
            jnp.zeros((heads_here, BLOCK), jnp.float32),
            jnp.zeros((BLOCK, heads_here, HEAD_DIM), jnp.float32),
        )
        peak, total, accum = lax.fori_loop(lowest, highest + 1, forward, start_state)
        safe_total = jnp.where(valid_block[None, :], total, 1.0)
        out_block = accum / jnp.transpose(safe_total)[:, :, None]
        out_block = jnp.where(valid_block[:, None, None], out_block, 0.0)
        log_total = jnp.where(valid_block[None, :], peak + jnp.log(safe_total), 0.0)
        row_dots = jnp.transpose(jnp.sum(grad_block * out_block, axis=2))

        def backward(tile_index, state):
            dq_block, dk_running, dv_running = state
            key_tile, value_tile, allowed, scores = tile_scores(tile_index)
            probs = jnp.where(
                allowed, jnp.exp(jnp.where(allowed, scores, 0.0) - log_total[:, :, None]), 0.0
            )
            dv_tile = jnp.einsum("hqk,qhd->khd", probs, grad_block, precision=HIGHEST_PRECISION)
            dp_tile = jnp.einsum(
                "qhd,khd->hqk", grad_block, value_tile, precision=HIGHEST_PRECISION
            )
            ds_tile = probs * (dp_tile - row_dots[:, :, None]) * scale
            dq_block = dq_block + jnp.einsum(
                "hqk,khd->qhd", ds_tile, key_tile, precision=HIGHEST_PRECISION
            )
            dk_tile = jnp.einsum("hqk,qhd->khd", ds_tile, query_block, precision=HIGHEST_PRECISION)
            dk_running = lax.dynamic_update_slice_in_dim(
                dk_running,
                block_rows(dk_running, tile_index) + dk_tile.reshape(BLOCK, width_dev),
                tile_index * BLOCK,
                0,
            )
            dv_running = lax.dynamic_update_slice_in_dim(
                dv_running,
                block_rows(dv_running, tile_index) + dv_tile.reshape(BLOCK, width_dev),
                tile_index * BLOCK,
                0,
            )
            return (dq_block, dk_running, dv_running)

        dq_block, dk_all, dv_all = lax.fori_loop(
            lowest,
            highest + 1,
            backward,
            (jnp.zeros((BLOCK, heads_here, HEAD_DIM), jnp.float32), dk_all, dv_all),
        )
        out_all = lax.dynamic_update_slice_in_dim(
            out_all, out_block.reshape(BLOCK, width_dev), block_index * BLOCK, 0
        )
        dq_all = lax.dynamic_update_slice_in_dim(
            dq_all, dq_block.reshape(BLOCK, width_dev), block_index * BLOCK, 0
        )
        return (out_all, dq_all, dk_all, dv_all)

    zeros_all = jnp.zeros((work_rows, width_dev), jnp.float32)
    return lax.fori_loop(0, block_count, one_block, (zeros_all, zeros_all, zeros_all, zeros_all))


def body(patches, in_projection, cotangent, image_lengths):
    patch_rows = jnp.transpose(patches)
    upstream = jnp.transpose(cotangent)
    row_count, width_dev = patch_rows.shape
    capacity = row_count // 4
    padded_room = (capacity + BLOCK - 1) // BLOCK * BLOCK
    extra_rows = padded_room - capacity
    partner_bit = lax.axis_size("dp").bit_length() - 2
    image_starts, row_begin, row_finish = image_bounds(image_lengths, row_count)
    image_load = jnp.sum(image_lengths * image_lengths)
    is_heavy = image_load * 8 > row_count * row_count
    tail_start = jnp.min(
        jnp.where(
            (image_starts >= row_count - capacity) & (image_lengths > 0), image_starts, row_count
        )
    )
    window_length = jnp.where(is_heavy, row_count - tail_start, 0)
    window_start = row_count - window_length
    query_from = jnp.zeros((), jnp.int32)
    positions = jnp.arange(row_count, dtype=jnp.int32)
    slot_index = jnp.arange(capacity, dtype=jnp.int32)
    in_window = slot_index < window_length
    query_slot = in_window & (slot_index >= query_from)
    keep_rows = jnp.logical_not(
        (positions >= window_start) & (positions < window_start + window_length)
    )

    def outbound(array):
        padded = jnp.concatenate(
            [array, jnp.zeros((capacity,) + array.shape[1:], array.dtype)], axis=0
        )
        piece = lax.dynamic_slice_in_dim(padded, window_start, capacity, 0)
        shaped_mask = in_window.reshape((capacity,) + (1,) * (array.ndim - 1))
        return jnp.where(shaped_mask, piece, jnp.zeros_like(piece))

    bounds_out = jnp.stack(
        [
            jnp.where(in_window, outbound(row_begin) - window_start, slot_index),
            jnp.where(in_window, outbound(row_finish) - window_start, slot_index + 1),
            query_slot.astype(jnp.int32),
        ]
    )

    def extend(own_rows, arrived_rows):
        return jnp.concatenate(
            [own_rows, arrived_rows, jnp.zeros((extra_rows,) + own_rows.shape[1:], own_rows.dtype)],
            axis=0,
        )

    arrived, marks_in = from_partner(
        (jnp.stack([outbound(patch_rows), outbound(upstream)]), bounds_out), "dp", partner_bit
    )
    whole_rows = gather_features(extend(patch_rows, arrived[0]))
    projected = project(whole_rows, in_projection)
    query_all = projected[:, :width_dev]
    key_all = projected[:, width_dev : 2 * width_dev]
    value_all = projected[:, 2 * width_dev :]
    grad_all = extend(upstream, arrived[1])
    pad_index = jnp.arange(row_count + capacity, row_count + padded_room, dtype=jnp.int32)
    work_begin = jnp.concatenate([row_begin, marks_in[0] + row_count, pad_index])
    work_finish = jnp.concatenate([row_finish, marks_in[1] + row_count, pad_index + 1])
    work_valid = jnp.concatenate([keep_rows, marks_in[2] > 0, jnp.zeros((extra_rows,), jnp.bool_)])
    out_all, dq_all, dk_all, dv_all = attend_blocks(
        query_all, key_all, value_all, grad_all, work_begin, work_finish, work_valid
    )
    results = jnp.stack([out_all, dq_all, dk_all, dv_all])
    returned = from_partner(results[:, row_count : row_count + capacity], "dp", partner_bit)
    zero_rows = jnp.zeros((4, row_count, width_dev), jnp.float32)
    padded_back = jnp.concatenate([zero_rows, returned, zero_rows], axis=1)
    placed = lax.dynamic_slice_in_dim(padded_back, row_count - window_start, row_count, 1)
    merged = results[:, :row_count] + placed
    grad_rows_all = jnp.concatenate([dq_all, dk_all, dv_all], axis=1)
    weight_gradient = lax.psum_scatter(
        lax.dot_general(
            whole_rows,
            grad_rows_all,
            (((0,), (0,)), ((), ())),
            precision=HIGHEST_PRECISION,
            preferred_element_type=jnp.float32,
        ),
        "dp",
        scatter_dimension=0,
        tiled=True,
    ).reshape(in_projection.shape)
    return (jnp.transpose(merged[0]), jnp.transpose(merged[1:4], (0, 2, 1)), weight_gradient)


def split(value):
    high = value.astype(jnp.bfloat16)
    return high, (value - high.astype(jnp.float32)).astype(jnp.bfloat16)


def dot(left, right, left_dim, right_dim):
    return lax.dot_general(
        left,
        right,
        (((left_dim,), (right_dim,)), ((), ())),
        preferred_element_type=jnp.float32,
    )


def in_vmem(count):
    return [pl.BlockSpec(memory_space=pltpu.VMEM)] * count


def whole_call(kernel, shapes, ids, arrays, flops, name):
    single = not isinstance(shapes, (list, tuple))
    outs = (shapes,) if single else tuple(shapes)
    moved = sum(a.size * a.dtype.itemsize for a in (*arrays, *outs))
    return pl.pallas_call(
        kernel,
        out_shape=shapes if single else outs,
        in_specs=[pl.BlockSpec(memory_space=pltpu.SMEM)] + in_vmem(len(arrays)),
        out_specs=in_vmem(1)[0] if single else tuple(in_vmem(len(outs))),
        cost_estimate=pl.CostEstimate(flops=flops, bytes_accessed=moved, transcendentals=0),
        compiler_params=pltpu.CompilerParams(vmem_limit_bytes=VMEM_LIMIT),
        name=name,
    )(ids, *arrays)


def f32(*shape):
    return jax.ShapeDtypeStruct(shape, jnp.float32)


def pack_kernel(ids, w_ref, own_ref, core_ref, pair_ref, scratch):
    me = ids[1] * 2 + ids[2]
    wide = w_ref.shape[2] // 4
    pieces = wide // HEAD_DIM
    for i in range(4):
        scratch[i] = jnp.concatenate(
            [
                w_ref[c, :, i * wide + a * HEAD_DIM : i * wide + (a + 1) * HEAD_DIM]
                for a in range(pieces)
                for c in range(3)
            ],
            axis=1,
        )
    own_ref[...] = scratch[me]
    core_ref[...] = scratch[me ^ 1]
    pair_ref[0] = scratch[me ^ 2]
    pair_ref[1] = scratch[me ^ 3]


def pack(ids, weight):
    _, rows, width = weight.shape
    cols = 3 * width // 4
    return pl.pallas_call(
        pack_kernel,
        out_shape=(f32(rows, cols), f32(rows, cols), f32(2, rows, cols)),
        in_specs=[pl.BlockSpec(memory_space=pltpu.SMEM)] + in_vmem(1),
        out_specs=tuple(in_vmem(3)),
        scratch_shapes=[pltpu.VMEM((4, rows, cols), jnp.float32)],
        compiler_params=pltpu.CompilerParams(vmem_limit_bytes=VMEM_LIMIT),
        cost_estimate=pl.CostEstimate(flops=0, bytes_accessed=weight.size * 8, transcendentals=0),
        name="pack",
    )(ids, weight)


def unpack_kernel(ids, *refs):
    pieces, out_ref, scratch = refs[:4], refs[4], refs[5]
    me = ids[1] * 2 + ids[2]
    wide = out_ref.shape[2] // 4
    heads = wide // HEAD_DIM
    for r in range(4):
        scratch[me ^ r] = pieces[r][...]
    for c in range(3):
        out_ref[c] = jnp.concatenate(
            [
                scratch[i, :, (a * 3 + c) * HEAD_DIM : (a * 3 + c + 1) * HEAD_DIM]
                for i in range(4)
                for a in range(heads)
            ],
            axis=1,
        )


def unpack(ids, pieces):
    rows, cols = pieces[0].shape
    return pl.pallas_call(
        unpack_kernel,
        out_shape=f32(3, rows, cols * 4 // 3),
        in_specs=[pl.BlockSpec(memory_space=pltpu.SMEM)] + in_vmem(4),
        out_specs=in_vmem(1)[0],
        scratch_shapes=[pltpu.VMEM((4, rows, cols), jnp.float32)],
        compiler_params=pltpu.CompilerParams(vmem_limit_bytes=VMEM_LIMIT),
        cost_estimate=pl.CostEstimate(
            flops=0, bytes_accessed=rows * cols * 32, transcendentals=0
        ),
        name="unpack",
    )(ids, *pieces)


def halves_kernel(ids, own_ref, other_ref, out_ref):
    half = own_ref.shape[0]
    for ref, side in ((own_ref, ids[3]), (other_ref, 1 - ids[3])):
        at = pl.multiple_of(side * half, 16)
        high, low = split(ref[...])
        out_ref[0, pl.ds(at, half), :] = high
        out_ref[1, pl.ds(at, half), :] = low


def halves(ids, own, other):
    half, rows = own.shape
    shape = jax.ShapeDtypeStruct((2, 2 * half, rows), jnp.bfloat16)
    return whole_call(halves_kernel, shape, ids, (own, other), own.size * 8, "halves")


def part_rows(ids, ring, shift, pair, core, depth):
    block = lax.rem(ids[0] + (shift + ring), ring)
    index = block * 4 + (ids[1] ^ pair) * 2 + (ids[2] ^ core)
    return pl.multiple_of(index * depth, 16)


def stack3(value):
    high, low = split(value)
    return jnp.concatenate([high, low, high], axis=0)


def part_product(ids, ring, shift, pair, w_ref, x_ref):
    depth = w_ref.shape[1]
    weights = [stack3(w_ref[core]) for core in range(2)]
    rows = []
    for core in range(2):
        at = part_rows(ids, ring, shift, pair, core, depth)
        high = x_ref[0, pl.ds(at, depth), :]
        low = x_ref[1, pl.ds(at, depth), :]
        rows.append(jnp.concatenate([high, high, low], axis=0))
    return dot(jnp.concatenate(weights, axis=0), jnp.concatenate(rows, axis=0), 0, 0)


def project_kernel(ring, where, ids, *refs):
    count = len(where)
    w_refs, x_refs, out_refs = refs[:count], refs[count : count + 4], refs[count + 4 :]
    for x_ref, out_ref in zip(x_refs, out_refs):
        total = None
        for (shift, pair), w_ref in zip(where, w_refs):
            term = part_product(ids, ring, shift, pair, w_ref, x_ref)
            total = term if total is None else total + term
        out_ref[...] = total


def attend_kernel(ring, where, scale, ids, seg_ref, w_ref, g_ref, p0, p1, x0, x1, out_ref):
    shift, pair = where
    for j, (p_ref, x_ref) in enumerate(((p0, x0), (p1, x1))):
        rows = p_ref.shape[1]
        p_ref_value = p_ref[...] + part_product(ids, ring, shift, pair, w_ref, x_ref)
        segment = jnp.broadcast_to(seg_ref[j], (rows, rows))
        same = segment == jnp.transpose(segment)
        for a in range(g_ref.shape[1]):
            base = a * 3 * HEAD_DIM
            query = p_ref_value[base : base + HEAD_DIM] * scale
            key = p_ref_value[base + HEAD_DIM : base + 2 * HEAD_DIM]
            value = p_ref_value[base + 2 * HEAD_DIM : base + 3 * HEAD_DIM]
            grad = g_ref[j, a]
            q_hi, q_lo = split(query)
            k_hi, k_lo = split(key)
            v_hi, v_lo = split(value)
            g_hi, g_lo = split(grad)
            scores = dot(
                jnp.concatenate([k_hi, k_lo, k_hi], axis=0),
                jnp.concatenate([q_hi, q_hi, q_lo], axis=0),
                0,
                0,
            )
            scores = jnp.where(same, scores, MASKED_SCORE)
            powers = jnp.exp(scores - jnp.max(scores, axis=0, keepdims=True))
            probs = powers * (1.0 / jnp.sum(powers, axis=0, keepdims=True))
            p_hi, p_lo = split(probs)

            def times(hi, lo, r_hi, r_lo, dim):
                both = dot(jnp.concatenate([hi, lo], axis=0), r_hi, 1, dim)
                return both[:HEAD_DIM] + both[HEAD_DIM:] + dot(hi, r_lo, 1, dim)

            mixed = times(v_hi, v_lo, p_hi, p_lo, 0)
            out_ref[j, a, 3] = mixed
            out_ref[j, a, 2] = times(g_hi, g_lo, p_hi, p_lo, 1)
            slopes = dot(
                jnp.concatenate([v_hi, v_lo, v_hi], axis=0),
                jnp.concatenate([g_hi, g_hi, g_lo], axis=0),
                0,
                0,
            )
            slopes = probs * (slopes - jnp.sum(grad * mixed, axis=0, keepdims=True))
            s_hi, s_lo = split(slopes)
            out_ref[j, a, 0] = times(k_hi, k_lo, s_hi, s_lo, 0) * scale
            out_ref[j, a, 1] = times(q_hi, q_lo, s_hi, s_lo, 1)


def weight_kernel(ring, where, ids, d0, d1, x00, x01, x10, x11, *out_refs):
    depth = out_refs[0].shape[1]
    heads = d0.shape[1]
    x_refs = ((x00, x01), (x10, x11))
    d_refs = (d0, d1)
    totals = [[None, None] for _ in where]
    for s in range(2):
        for j in range(2):
            grads = jnp.concatenate(
                [d_refs[s][j, a, c] for a in range(heads) for c in range(3)], axis=0
            )
            d_hi, d_lo = split(grads)
            for n, (shift, pair) in enumerate(where):
                for core in range(2):
                    at = part_rows(ids, ring, shift, pair, core, depth)
                    high = x_refs[s][j][0, pl.ds(at, depth), :]
                    low = x_refs[s][j][1, pl.ds(at, depth), :]
                    both = dot(jnp.concatenate([high, low], axis=0), d_hi, 1, 1)
                    term = both[:depth] + both[depth:] + dot(high, d_lo, 1, 1)
                    old = totals[n][core]
                    totals[n][core] = term if old is None else old + term
    for n, out_ref in enumerate(out_refs):
        for core in range(2):
            out_ref[core] = totals[n][core]


def place_kernel(ids, r0, r1, r2, r3, mixed_ref, grads_ref):
    me = ids[1] * 2 + ids[2]
    heads = r0.shape[1]
    for r, (ref, j) in enumerate(((r0, 0), (r1, 0), (r2, 0), (r3, 1))):
        for a in range(heads):
            at = pl.multiple_of(((me ^ r) * heads + a) * HEAD_DIM, 8)
            mixed_ref[pl.ds(at, HEAD_DIM), :] = ref[j, a, 3]
            for c in range(3):
                grads_ref[c, pl.ds(at, HEAD_DIM), :] = ref[j, a, c]


def swap(value, axis):
    return lax.ppermute(value, axis, [(0, 1), (1, 0)])


def turn(value, step):
    ring = lax.axis_size("ring")
    return lax.ppermute(value, "ring", [(i, (i + step) % ring) for i in range(ring)])


def fast_body(patches, in_projection, cotangent, image_lengths):
    ring = lax.axis_size("ring")
    width, rows = patches.shape
    depth = in_projection.shape[0]
    heads = width // HEAD_DIM // 4
    wide = heads * HEAD_DIM
    scale = HEAD_DIM ** (-0.5)
    pair_at, core_at = lax.axis_index("pair"), lax.axis_index("core")
    ids = jnp.stack(
        [lax.axis_index("ring"), pair_at, core_at, lax.axis_index("tensor")]
    ).astype(jnp.int32)
    me = pair_at * 2 + core_at

    w_own, w_core, w_pair = pack(ids, jnp.transpose(in_projection, (1, 0, 2)))
    near = jnp.stack([w_own, swap(w_core, "core")])
    parts = {(0, 0): near}
    parts[-1, 0] = turn(near, 1)
    parts[1, 0] = turn(near, -1)
    w_far = swap(w_pair, "pair")
    far = jnp.stack([w_far[0], swap(w_far[1], "core")])
    parts[0, 1] = far
    parts[1, 1] = turn(far, -1)
    parts[-1, 1] = turn(far, 1)
    parts[-2, 0] = turn(parts[-1, 0], 1)
    last = turn(parts[1, 1], -1)
    last_where = (2, 1)

    x_pair = swap(patches, "pair")
    x_tensor = swap(patches, "tensor")
    x_both = swap(x_pair, "tensor")
    x_rows = [
        halves(ids, patches, x_tensor),
        halves(ids, swap(patches, "core"), swap(x_tensor, "core")),
        halves(ids, x_pair, x_both),
        halves(ids, swap(x_pair, "core"), swap(x_both, "core")),
    ]

    steps = jnp.arange(image_lengths.shape[0], dtype=jnp.int32)
    ends = jnp.sum(jnp.where(steps[None, :] <= steps[:, None], image_lengths[None, :], 0), axis=1)
    places = jnp.arange(rows, dtype=jnp.int32)
    image = jnp.sum((places[None, :] >= ends[:, None]).astype(jnp.float32), axis=0)[None]
    image_pair = swap(image, "pair")
    image_a = jnp.stack([image, image_pair])
    image_b = swap(image_a, "core")

    def grad_heads(array, index):
        return lax.dynamic_slice_in_dim(array, index * wide, wide, 0)

    g_pair = swap(lax.dynamic_slice_in_dim(cotangent, (1 - pair_at) * 2 * wide, 2 * wide, 0), "pair")
    shape = (2, heads, HEAD_DIM, rows)
    grad_a = jnp.stack([grad_heads(cotangent, me), grad_heads(g_pair, core_at)]).reshape(shape)
    grad_b = swap(
        jnp.stack([grad_heads(cotangent, me ^ 1), grad_heads(g_pair, 1 - core_at)]), "core"
    ).reshape(shape)

    where = tuple(parts)
    flops = 2 * 3 * 3 * wide * 2 * depth * rows
    partial = whole_call(
        functools.partial(project_kernel, ring, where),
        [f32(3 * wide, rows)] * 4,
        ids,
        (*parts.values(), *x_rows),
        flops * 4 * len(where),
        "project",
    )

    def attend(images, grads, indices, name):
        return whole_call(
            functools.partial(attend_kernel, ring, last_where, scale),
            f32(2, heads, 4, HEAD_DIM, rows),
            ids,
            (
                images,
                last,
                grads,
                *(partial[i] for i in indices),
                *(x_rows[i] for i in indices),
            ),
            2 * flops + 2 * heads * 7 * 6 * HEAD_DIM * rows * rows,
            name,
        )

    done_b = attend(image_b, grad_b, (1, 3), "attend_b")
    done_a = attend(image_a, grad_a, (0, 2), "attend_a")

    def weight_parts(name, *where):
        return whole_call(
            functools.partial(weight_kernel, ring, where),
            [f32(2, depth, 3 * wide)] * len(where),
            ids,
            (done_a, done_b, x_rows[0], x_rows[2], x_rows[1], x_rows[3]),
            flops * 4 * len(where),
            name,
        )

    far_two, far_side = weight_parts("weight_far", (-2, 1), (1, 1))
    far_chain = turn(far_two, -1)
    far_direct = turn(far_side, 1)
    near_two, near_side = weight_parts("weight_near", (2, 0), (-1, 0))
    near_chain = turn(near_two, 1)
    near_direct = turn(near_side, -1)
    far_mid, near_mid, far_own, near_own = weight_parts(
        "weight_rest", (-1, 1), (1, 0), (0, 1), (0, 0)
    )
    far_chain = turn(far_chain + far_mid, -1)
    near_chain = turn(near_chain + near_mid, 1)
    far_sum = swap(far_own + far_direct + far_chain, "pair")
    near_sum = near_own + near_direct + near_chain
    pieces = [near_sum[0], swap(near_sum[1], "core"), far_sum[0], swap(far_sum[1], "core")]
    weight_gradient = jnp.transpose(unpack(ids, pieces), (1, 0, 2))

    back_core = swap(done_b, "core")
    back_pair = swap(jnp.stack([done_a[1], back_core[1]]), "pair")
    mixed, grads = whole_call(
        place_kernel,
        [f32(width, rows), f32(3, width, rows)],
        ids,
        (done_a, back_core, back_pair, back_pair),
        0,
        "place",
    )
    return mixed, grads, weight_gradient


def solution(mesh):
    ring = mesh.shape["dp"] // 4
    tensor = mesh.shape["tensor"]

    def run(patches, in_projection, cotangent, image_lengths):
        width = patches.shape[0] // tensor
        rows = patches.shape[1] // mesh.shape["dp"]
        depth = in_projection.shape[0] // mesh.shape["dp"]
        fits = (
            ring == 4
            and tensor == 2
            and width % (4 * HEAD_DIM) == 0
            and depth % 16 == 0
            and rows % BLOCK == 0
        )
        dp, over, inner = "dp", mesh, body
        if fits:
            dp, inner = ("ring", "pair", "core"), fast_body
            over = jax.sharding.Mesh(
                mesh.devices.reshape(ring, 2, 2, tensor), (*dp, "tensor")
            )
        return jax.shard_map(
            inner,
            mesh=over,
            in_specs=(P("tensor", dp), P(dp, None, "tensor"), P("tensor", dp), P(dp)),
            out_specs=(P("tensor", dp), P(None, "tensor", dp), P(dp, None, "tensor")),
            check_vma=False,
        )(patches, in_projection, cotangent, image_lengths)

    return run
```
